32 devices in a mesh: pix: 8 (over z, y), rep: 4 (over x, core).
Axes of the slice: x: 2, y: 2, z: 4, core: 2. Of those that a mesh axis runs over, the one named last changes fastest.
Arguments:
- sky_cube: float32 [4, 512, 65536], P('rep', None, 'pix'), may hold values from -6 to 10
- pixel_mask: int32 [4, 65536], P('rep', 'pix'), may hold values 0 or 1
- noise_cov: float32 [512, 512], replicated, may hold values from -1 to 2, as said below
Outputs:
- power_cube: float32 [4, 512, 65536], P('rep', 'pix')
The draws below stay inside these ranges and needn't reach their ends.
Inputs may be any that keep to these rules, and one draw needn't show every extreme that they name: `noise_cov`: symmetric; each diagonal entry exceeds the sum of magnitudes off the diagonal in its row.
All inputs are finite; a program needn't handle non-finite values. No bound on the sum of `pixel_mask` on one device may be relied on, other than what follows from the above.
Results may differ from the reference program's by a relative error of at most 0.00012.
Values sent between devices are 32-bit elements; how exact they have to be, the bound alone decides.
A program may use at most 320 MiB of HBM per device.

```python
import math
import jax
import jax.numpy as jnp
from jax import lax

F = 512
SY = 256
SX = 256
PIX = 65536
PATCHES = 4


def draw_sky_cube(key, part):
    keys = jax.random.split(key, 5)
    shape_pix = (PATCHES, 1, PIX)
    chan = (1.0 + jnp.arange(F, dtype=jnp.float32) / F)[None, :, None]
    amp_sync = jnp.exp(jax.random.uniform(keys[0], shape_pix, jnp.float32, math.log(0.5), math.log(3.0)))
    beta_sync = jax.random.uniform(keys[1], shape_pix, jnp.float32, 2.5, 3.1)
    amp_free = jnp.exp(jax.random.uniform(keys[2], shape_pix, jnp.float32, math.log(0.2), math.log(1.0)))
    beta_free = jax.random.uniform(keys[3], shape_pix, jnp.float32, 2.0, 2.2)
    noise = jax.random.truncated_normal(keys[4], -6.0, 6.0, (PATCHES, F, PIX), jnp.float32)
    fore = amp_sync * jnp.exp(-beta_sync * jnp.log(chan)) + amp_free * jnp.exp(-beta_free * jnp.log(chan))
    return (fore + noise).astype(jnp.float32)


def draw_noise_cov(key, part):
    keys = jax.random.split(key, 2)
    diag_vals = jnp.exp(jax.random.uniform(keys[0], (F,), jnp.float32, 0.0, math.log(2.0)))
    off = jax.random.uniform(keys[1], (F, F), jnp.float32, -0.9 / F, 0.9 / F)
    off = (off + off.T) * 0.5
    idx = jnp.arange(F, dtype=jnp.int32)
    ident = (idx[:, None] == idx[None, :]).astype(jnp.float32)
    return (off * (1.0 - ident) + ident * diag_vals[None, :]).astype(jnp.float32)


def with_ends(values, stream_key, smallest, top_value):
    spot = [jax.random.randint(jax.random.fold_in(stream_key, axis), (), 0, length) for axis, length in enumerate(values.shape)]
    widest = values.shape.index(max(values.shape))
    beside = spot[:widest] + [(spot[widest] + 1) % values.shape[widest]] + spot[widest + 1:]
    return values.at[tuple(spot)].set(smallest).at[tuple(beside)].set(top_value)


def setup_inputs(seed: int = 0) -> dict:
    seeds = jax.random.split(jax.random.key(seed), 4)
    return {
        "sky_cube": draw_sky_cube(jax.random.fold_in(seeds[3], 71), 0),
        "pixel_mask": with_ends((jax.random.randint(seeds[1], (PATCHES, PIX), 0, 10) < 9).astype(jnp.int32), jax.random.fold_in(seeds[1], 1), 0, 1),
        "noise_cov": draw_noise_cov(jax.random.fold_in(seeds[3], 71), 0),
    }


HI = lax.Precision.HIGHEST

def dft_pair(length):
    idx = jnp.arange(length, dtype=jnp.int32)
    phase = (idx[:, None] * idx[None, :] % length).astype(jnp.float32) * (2.0 * math.pi / length)
    return (jnp.cos(phase), jnp.sin(phase))

def los_table(length):
    idx = jnp.arange(length, dtype=jnp.int32)
    half_len = length // 2
    freq = jnp.where(idx <= half_len, idx, idx - half_len)
    phase = (freq[:, None] * idx[None, :] % length).astype(jnp.float32) * (2.0 * math.pi / length)
    values = jnp.where((idx <= half_len)[:, None], jnp.cos(phase), jnp.sin(phase))
    edge = jnp.logical_or(idx == 0, idx == half_len)
    scale = jnp.where(edge, math.sqrt(1.0 / length), math.sqrt(2.0 / length)).astype(jnp.float32)
    return values * scale[:, None]

def sky_power(planes, rows_y, cols_x):
    count = planes.shape[0]
    field = planes.reshape(count, rows_y, cols_x)
    cos_x, sin_x = dft_pair(cols_x)
    cos_y, sin_y = dft_pair(rows_y)
    both_x = jnp.concatenate([cos_x, sin_x], axis=1)
    both_y = jnp.concatenate([cos_y, sin_y], axis=0)
    first = jnp.einsum('kyx,xw->kyw', field, both_x, precision=HI)
    second = jnp.einsum('vy,kyw->kvw', both_y, first, precision=HI)
    real_part = second[:, :rows_y, :cols_x] - second[:, rows_y:, cols_x:]
    imag_part = -(second[:, rows_y:, :cols_x] + second[:, :rows_y, cols_x:])
    power_map = (real_part * real_part + imag_part * imag_part) / float(rows_y * cols_x)
    return power_map.reshape(count, rows_y * cols_x)

def reference(sky_cube, pixel_mask, noise_cov):
    live = pixel_mask.astype(jnp.float32)[:, None, :]
    masked = sky_cube * live

    def patch_cov(patch):
        return jnp.dot(patch, patch.T, precision=HI)
    data_cov = lax.optimization_barrier(jnp.sum(lax.map(patch_cov, masked), axis=0))
    regular = data_cov / float(PATCHES * PIX) + noise_cov
    factor = jnp.linalg.cholesky(regular)
    filter_t = jax.scipy.linalg.cho_solve((factor, True), noise_cov)
    table = los_table(F)

    def patch_power(patch):
        cleaned = jnp.dot(filter_t.T, patch, precision=HI)
        spectra = jnp.dot(table, cleaned, precision=HI)
        groups = spectra.reshape(F // 8, 8, PIX)
        result = lax.map(lambda planes: sky_power(planes, SY, SX), groups)
        return result.reshape(F, PIX)
    return lax.map(patch_power, masked)
```

```python
import functools
import math

import jax
import jax.numpy as jnp
import numpy as np
from jax import lax
from jax.experimental import pallas as pl
from jax.experimental.pallas import tpu as pltpu
from jax.sharding import PartitionSpec as P

F = 512
SY = 256
SX = 256
BLOCK = 128

HI = lax.Precision.HIGHEST
MID = lax.Precision.HIGH
MESH = pl.DeviceIdType.MESH


def dft_pair(length):
    idx = jnp.arange(length, dtype=jnp.int32)
    phase = (idx[:, None] * idx[None, :] % length).astype(jnp.float32) * (2.0 * math.pi / length)
    return (jnp.cos(phase), jnp.sin(phase))


def los_table(length):
    idx = np.arange(length)
    half_len = length // 2
    freq = np.where(idx <= half_len, idx, idx - half_len)
    phase = (freq[:, None] * idx[None, :] % length) * (2.0 * math.pi / length)
    values = np.where((idx <= half_len)[:, None], np.cos(phase), np.sin(phase))
    edge = np.logical_or(idx == 0, idx == half_len)
    scale = np.where(edge, math.sqrt(1.0 / length), math.sqrt(2.0 / length))
    return (values * scale[:, None]).astype(np.float32)


def sky_power(planes, rows_y, cols_x):
    count = planes.shape[0]
    field = planes.reshape(count, rows_y, cols_x)
    cos_x, sin_x = dft_pair(cols_x)
    cos_y, sin_y = dft_pair(rows_y)
    both_x = jnp.concatenate([cos_x, sin_x], axis=1)
    both_y = jnp.concatenate([cos_y, sin_y], axis=0)
    first = jnp.einsum("kyx,xw->kyw", field, both_x, precision=MID)
    second = jnp.einsum("vy,kyw->kvw", both_y, first, precision=MID)
    real_part = second[:, :rows_y, :cols_x] - second[:, rows_y:, cols_x:]
    imag_part = -(second[:, rows_y:, :cols_x] + second[:, :rows_y, cols_x:])
    power_map = (real_part * real_part + imag_part * imag_part) / float(rows_y * cols_x)
    return power_map.reshape(count, rows_y * cols_x)


def sum_kernel(axes, x_ref, o_ref, acc, full, got, send_sem, recv_sem):
    where = {name: lax.axis_index(name) for name, _ in axes}
    steps = []
    for name, size in axes:
        bit = 1
        while bit < size:
            steps.append((name, bit))
            bit *= 2

    def partner(name, bit):
        me = where[name]
        mine = lax.rem(me // bit, 2)
        return mine, {name: me + bit * (1 - 2 * mine)}

    barrier = pltpu.get_barrier_semaphore()
    for name, bit in steps:
        _, other = partner(name, bit)
        pl.semaphore_signal(barrier, inc=1, device_id=other, device_id_type=MESH)
    pl.semaphore_wait(barrier, len(steps))

    total = x_ref.shape[0]
    rows, start, offset = total, 0, 0
    acc[...] = x_ref[...]
    plan = []
    for n, (name, bit) in enumerate(steps):
        mine, other = partner(name, bit)
        split = rows % 16 == 0
        if split:
            rows //= 2
            away = start + (1 - mine) * rows
            start = start + mine * rows
        else:
            away = start
        plan.append((other, split, start, rows, mine))
        if split:
            away = pl.multiple_of(away, 8)
        here = pl.multiple_of(start, 8)
        source = x_ref if n == 0 else acc
        copy = pltpu.make_async_remote_copy(
            src_ref=source.at[pl.ds(away, rows)],
            dst_ref=got.at[pl.ds(offset, rows)],
            send_sem=send_sem.at[n],
            recv_sem=recv_sem.at[n],
            device_id=other,
            device_id_type=MESH,
        )
        copy.start()
        copy.wait()
        acc[pl.ds(here, rows)] = acc[pl.ds(here, rows)] + got[pl.ds(offset, rows)]
        offset += rows
    last = pl.ds(pl.multiple_of(start, 8), rows)
    full[last] = acc[last]
    for n in reversed(range(len(steps))):
        other, split, start, rows, mine = plan[n]
        if not split:
            continue
        here = pl.multiple_of(start, 8)
        copy = pltpu.make_async_remote_copy(
            src_ref=full.at[pl.ds(here, rows)],
            dst_ref=full.at[pl.ds(here, rows)],
            send_sem=send_sem.at[len(steps) + n],
            recv_sem=recv_sem.at[len(steps) + n],
            device_id=other,
            device_id_type=MESH,
        )
        copy.start()
        copy.wait()
    o_ref[...] = full[...]


def reduce_cov(partial_value, sizes):
    axes = [("rep", sizes["rep"]), ("pix", sizes["pix"])]
    rows, depth, count = partial_value.shape[0], 0, 0
    for _, size in axes:
        for _ in range(size.bit_length() - 1):
            if rows % 16 == 0:
                rows //= 2
            depth += rows
            count += 1
    vmem = pl.BlockSpec(memory_space=pltpu.VMEM)
    return pl.pallas_call(
        functools.partial(sum_kernel, axes),
        out_shape=jax.ShapeDtypeStruct(partial_value.shape, jnp.float32),
        in_specs=[vmem],
        out_specs=vmem,
        scratch_shapes=[
            pltpu.VMEM(partial_value.shape, jnp.float32),
            pltpu.VMEM(partial_value.shape, jnp.float32),
            pltpu.VMEM((depth, partial_value.shape[1]), jnp.float32),
            pltpu.SemaphoreType.DMA((2 * count,)),
            pltpu.SemaphoreType.DMA((2 * count,)),
        ],
        compiler_params=pltpu.CompilerParams(collective_id=0, has_side_effects=True),
        name="cov_sum",
    )(partial_value)


def block_inverse(a):
    size = a.shape[0]
    row_id = lax.broadcasted_iota(jnp.int32, (size, size), 0)
    col_id = lax.broadcasted_iota(jnp.int32, (size, size), 1)
    for j in range(size):
        pivot = 1.0 / a[j : j + 1, j : j + 1]
        row = a[j : j + 1, :] * pivot
        col = a[:, j : j + 1]
        base = jnp.where(col_id == j, 0.0, a)
        row = jnp.where(col_id[:1] == j, pivot, row)
        a = jnp.where(row_id == j, row, base - col * row)
    return a


def solve_kernel(scale, cov_ref, noise_ref, table_ref, o_ref, a_ref):
    size = cov_ref.shape[0]
    a_ref[...] = cov_ref[...] * scale + noise_ref[...]
    o_ref[...] = lax.dot_general(
        noise_ref[...],
        table_ref[...],
        (((1,), (1,)), ((), ())),
        precision=HI,
        preferred_element_type=jnp.float32,
    )
    blocks = size // BLOCK

    def mul(x, y):
        return jnp.dot(x, y, precision=HI, preferred_element_type=jnp.float32)

    def step(k, _):
        here = pl.ds(pl.multiple_of(k * BLOCK, BLOCK), BLOCK)
        inverse = block_inverse(a_ref[here, here])
        panel = mul(inverse, a_ref[here, :])
        right = mul(inverse, o_ref[here, :])
        for i in range(blocks):
            rows = pl.ds(i * BLOCK, BLOCK)

            @pl.when(k != i)
            def _():
                factor = a_ref[rows, here]
                o_ref[rows, :] = o_ref[rows, :] - mul(factor, right)

                @pl.when(k < blocks - 1)
                def _():
                    a_ref[rows, :] = a_ref[rows, :] - mul(factor, panel)

        o_ref[here, :] = right
        a_ref[here, :] = panel
        return 0

    lax.fori_loop(0, blocks, step, 0)


def folded_transpose(data_cov, scale, noise_cov, table):
    vmem = pl.BlockSpec(memory_space=pltpu.VMEM)
    return pl.pallas_call(
        functools.partial(solve_kernel, scale),
        out_shape=jax.ShapeDtypeStruct(data_cov.shape, jnp.float32),
        in_specs=[vmem] * 3,
        out_specs=vmem,
        scratch_shapes=[pltpu.VMEM(data_cov.shape, jnp.float32)],
        name="filter_solve",
    )(data_cov, noise_cov, table)


def local(sizes, sky_cube, pixel_mask, noise_cov):
    live = pixel_mask[0].astype(jnp.float32)
    masked = sky_cube[0] * live[None, :]
    table = jnp.asarray(los_table(F))
    partial_value = jnp.dot(masked, masked.T, precision=MID)
    data_cov = reduce_cov(partial_value, sizes)
    count_all = sizes["pix"] * sizes["rep"] * masked.shape[1]
    folded = folded_transpose(data_cov, 1.0 / count_all, noise_cov, table).T
    owners = sizes["pix"]
    share = F // owners
    eighth = share // 8
    widths = [eighth, 2 * eighth, 2 * eighth, 2 * eighth, eighth] if eighth else [share]
    by_owner = folded.reshape(owners, share, F)
    result, planes = None, []

    def place(done, at, result):
        power = sky_power(planes[done][0], SY, SX)
        if result is None:
            return jnp.pad(power, ((at, share - at - power.shape[0]), (0, 0)))
        return lax.dynamic_update_slice(result, power, (at, 0))

    starts = [sum(widths[:c]) for c in range(len(widths))]
    for c, width in enumerate(widths):
        rows = by_owner[:, starts[c] : starts[c] + width].reshape(owners * width, F)
        spectra = jnp.dot(rows, masked, precision=MID)
        stacked = spectra.reshape(owners, width, spectra.shape[1])
        if c >= 2:
            result = place(c - 2, starts[c - 2], result)
            stacked, result = lax.optimization_barrier((stacked, result))
        planes.append(lax.all_to_all(stacked, "pix", split_axis=0, concat_axis=2, tiled=True))
    for done in range(max(0, len(widths) - 2), len(widths)):
        result = place(done, starts[done], result)
    return result[None]


def solution(mesh):
    placed = (P("rep", None, "pix"), P("rep", "pix"), P())
    return jax.shard_map(
        functools.partial(local, dict(mesh.shape)),
        mesh=mesh,
        in_specs=placed,
        out_specs=P("rep", "pix", None),
        check_vma=False,
    )
```
